512 devices in a mesh: row: 32 (over z, core), col: 16 (over y, x).
Axes of the slice: x: 4, y: 4, z: 16, core: 2. Of those that a mesh axis runs over, the one named last changes fastest.
Arguments:
- features: bfloat16 [16, 4096, 256], P('col', 'row'), may hold values from -6 to 6
- tiles: bfloat16 [32, 16, 56, 128, 128], P('row', 'col'), may hold values from -0.5 to 0.5
- tile_rows: int32 [32, 16, 56], P('row', 'col'), may hold values from 0 to 15, as said below
- tile_cols: int32 [32, 16, 56], P('row', 'col'), may hold values from 0 to 31, as said below
- tile_count: int32 [32, 16], P('row', 'col'), may hold values from 4 to 56, as said below
- weight: bfloat16 [256, 256], replicated, may hold values from -0.375 to 0.375
- bias: float32 [256], replicated, may hold values from -3 to 3
- cotangent: bfloat16 [32, 2048, 256], P('row', 'col'), may hold values from -6 to 6
- label_mask: int32 [32, 2048], P('row', 'col'), may hold values 0 or 1
Outputs:
- hidden: bfloat16 [32, 2048, 256], P('row', 'col')
- grad_weight: float32 [256, 256], replicated
- grad_bias: float32 [256], replicated
- grad_features: bfloat16 [16, 4096, 256], P('col', 'row')
The draws below stay inside these ranges and needn't reach their ends.
Inputs may be any that keep to these rules, and one draw needn't show every extreme that they name: `tile_rows`: tile row among the 16 tile rows of a block; the (row, column) positions of one block's slots are all distinct. `tile_cols`: tile column among the 32 tile columns of a block. The live slots of a block are its first tile_count slots; some block has all 56 slots live.
All inputs are finite; a program needn't handle non-finite values. No bound on the sum of `label_mask` on one device may be relied on, other than what follows from the above.
Results may differ from the reference program's by a relative error of at most 0.023.
Values may be sent and summed in bfloat16 or wider, within the bound.
A program may use at most 64 MiB of HBM per device.

```python
import math
import jax
import jax.numpy as jnp
from jax import lax

F = 256
TB = 128
RT = 1
R = 128
TMAX = 56
NODES = 65536
N_ROW = 32
N_COL = 16


def slot_positions(key):
    pattern_key = jax.random.fold_in(key, 11)
    positions = N_COL * RT * N_ROW * RT
    keys = jax.random.split(pattern_key, N_ROW * N_COL)
    picked = jax.vmap(lambda one_key: jax.random.permutation(one_key, positions)[:TMAX])(keys)
    return picked.reshape(N_ROW, N_COL, TMAX).astype(jnp.int32)


def draw_tile_rows(key, part):
    return slot_positions(key) // (N_ROW * RT)


def draw_tile_cols(key, part):
    return slot_positions(key) % (N_ROW * RT)


def draw_tile_count(key, part):
    count_key = jax.random.fold_in(key, 23)
    first_key, second_key, place_key = jax.random.split(count_key, 3)
    lowest = max(TMAX // 14, 1)
    spread_range = max(TMAX - lowest, 1)
    first = jax.random.randint(first_key, (N_ROW * N_COL,), 0, spread_range + 1)
    second = jax.random.randint(second_key, (N_ROW * N_COL,), 0, spread_range + 1)
    counts = jnp.minimum(lowest + first * second // spread_range, TMAX)
    place = jax.random.randint(place_key, (), 0, N_ROW * N_COL)
    counts = counts.at[place].set(TMAX)
    return counts.reshape(N_ROW, N_COL).astype(jnp.int32)


def with_ends(drawn, stream_key, least, top_value):
    spot = [jax.random.randint(jax.random.fold_in(stream_key, axis), (), 0, length) for axis, length in enumerate(drawn.shape)]
    longest = drawn.shape.index(max(drawn.shape))
    beside = spot[:longest] + [(spot[longest] + 1) % drawn.shape[longest]] + spot[longest + 1:]
    return drawn.at[tuple(spot)].set(least).at[tuple(beside)].set(top_value)


def block_scale(rng, extent, shards, least, largest):
    def one(dim, shards_of):
        heights = jax.random.uniform(jax.random.fold_in(jax.random.fold_in(rng, 6), dim), (shards_of,), jnp.float32, least / len(shards), largest / len(shards))
        return jnp.repeat(jnp.exp(heights), extent[dim] // shards_of).reshape((-1,) + (1,) * (len(extent) - dim - 1))

    factor_of = one(*shards[0])
    for cut in shards[1:]:
        factor_of = factor_of * one(*cut)
    return factor_of


def noise(rng, extent, width, reach, cuts=(), kind=jnp.bfloat16):
    array = width * jax.random.normal(rng, extent, jnp.float32)
    if cuts:
        array = array * block_scale(rng, extent, cuts, -0.22, 0.18)
    return jnp.clip(array, -reach, reach).astype(kind)


def setup_inputs(seed: int = 0) -> dict:
    key_of = jax.random.split(jax.random.key(seed), 10)
    return {
        "features": noise(key_of[0], (N_COL, N_ROW * R, F), 1.0, 6.0, ((0, 16), (1, 32))),
        "tiles": noise(key_of[1], (N_ROW, N_COL, TMAX, TB, TB), ((TMAX * N_COL) ** -0.5), 0.5, ((0, 32), (1, 16))),
        "tile_rows": draw_tile_rows(jax.random.fold_in(key_of[9], 71), 0),
        "tile_cols": draw_tile_cols(jax.random.fold_in(key_of[9], 71), 0),
        "tile_count": draw_tile_count(jax.random.fold_in(key_of[9], 71), 0),
        "weight": noise(key_of[5], (F, F), F ** -0.5, 0.375),
        "bias": noise(key_of[6], (F,), 0.5, 3.0, (), jnp.float32),
        "cotangent": noise(key_of[7], (N_ROW, N_COL * R, F), 1.0, 6.0, ((0, 32), (1, 16))),
        "label_mask": with_ends((jax.random.randint(key_of[8], (N_ROW, N_COL * R), 0, 3) < 1).astype(jnp.int32), jax.random.fold_in(key_of[8], 1), 0, 1),
    }


def spread(block_tiles, take_index, put_index, live_count, source, out_tiles, transpose):
    picked = source[take_index].astype(jnp.float32)
    block = block_tiles.astype(jnp.float32)
    if transpose:
        product = jnp.einsum('sij,sif->sjf', block, picked)
    else:
        product = jnp.einsum('sij,sjf->sif', block, picked)
    live = jnp.arange(block_tiles.shape[0], dtype=jnp.int32) < live_count
    product = jnp.where(live[:, None, None], product, jnp.float32(0.0))
    empty = jnp.zeros((out_tiles, TB, F), jnp.float32)
    return empty.at[put_index].add(product)

def reference(features, tiles, tile_rows, tile_cols, tile_count, weight, bias, cotangent, label_mask):
    col_tiles = N_ROW * R // TB
    row_tiles = N_COL * R // TB

    def forward_row(r_index):

        def step(total, c_index):
            source = features[c_index].reshape(col_tiles, TB, F)
            term = spread(tiles[r_index, c_index], tile_cols[r_index, c_index], tile_rows[r_index, c_index], tile_count[r_index, c_index], source, row_tiles, False)
            return (total + term, None)
        total, _ = lax.scan(step, jnp.zeros((row_tiles, TB, F), jnp.float32), jnp.arange(N_COL, dtype=jnp.int32))
        return total.reshape(N_COL * R, F)
    aggregated = lax.map(forward_row, jnp.arange(N_ROW, dtype=jnp.int32)).astype(jnp.bfloat16)
    flat = aggregated.reshape(NODES, F)
    pre_act = jnp.dot(flat, weight, preferred_element_type=jnp.float32) + bias
    sigma = jax.nn.sigmoid(pre_act)
    hidden = (pre_act * sigma).astype(jnp.bfloat16).reshape(N_ROW, N_COL * R, F)
    kept = label_mask.reshape(NODES).astype(jnp.float32)[:, None]
    slope = sigma * (1.0 + pre_act * (1.0 - sigma))
    grad_pre = (cotangent.reshape(NODES, F).astype(jnp.float32) * kept * slope).astype(jnp.bfloat16)
    scale = 1.0 / math.sqrt(NODES)
    grad_weight = jnp.dot(flat.T, grad_pre, preferred_element_type=jnp.float32) * scale
    grad_bias = lax.optimization_barrier(jnp.sum(grad_pre.astype(jnp.float32), axis=0)) * scale
    grad_agg = jnp.dot(grad_pre, weight.T, preferred_element_type=jnp.float32).astype(jnp.bfloat16).reshape(N_ROW, N_COL * R, F)

    def backward_col(c_index):

        def step(total, r_index):
            source = grad_agg[r_index].reshape(row_tiles, TB, F)
            term = spread(tiles[r_index, c_index], tile_rows[r_index, c_index], tile_cols[r_index, c_index], tile_count[r_index, c_index], source, col_tiles, True)
            term = lax.optimization_barrier(term.astype(jnp.bfloat16)).astype(jnp.float32)
            return (total + term, None)
        total, _ = lax.scan(step, jnp.zeros((col_tiles, TB, F), jnp.float32), jnp.arange(N_ROW, dtype=jnp.int32))
        return total.reshape(N_ROW * R, F)
    grad_features = lax.map(backward_col, jnp.arange(N_COL, dtype=jnp.int32)).astype(jnp.bfloat16)
    return (hidden, grad_weight, grad_bias, grad_features)
```

```python
import functools
import math

import jax
import jax.numpy as jnp
from jax import lax
from jax.experimental import pallas as pl
from jax.experimental.pallas import tpu as pltpu
from jax.sharding import PartitionSpec as P

MESH = pl.DeviceIdType.MESH
PARTS = 4
F32 = jnp.float32
BF16 = jnp.bfloat16


def order_rows(key, limit):
    size = key.shape[1]
    by_lane = jnp.broadcast_to(key, (size, size))
    by_sub = by_lane.T
    lane = lax.broadcasted_iota(jnp.int32, (size, size), 1)
    sub = lax.broadcasted_iota(jnp.int32, (size, size), 0)
    same_before = jnp.where(by_sub == by_lane, jnp.where(sub < lane, 1, 0), 0)
    before = jnp.where(by_sub < by_lane, 1, same_before)
    rank = jnp.sum(before, axis=0, keepdims=True)
    repeats = jnp.sum(same_before, axis=0, keepdims=True)
    rank_sub = jnp.broadcast_to(rank, (size, size)).T
    repeats_sub = jnp.broadcast_to(repeats, (size, size)).T
    here = rank_sub == lane
    slot = jnp.sum(jnp.where(here, sub, 0), axis=0, keepdims=True)
    first = jnp.sum(jnp.where(here, jnp.where(repeats_sub == 0, 1, 0), 0), axis=0, keepdims=True)
    last = jnp.sum(jnp.where(by_sub <= lane, 1, 0), axis=0, keepdims=True) - 1
    last = jnp.maximum(last, 0)
    present = jnp.sum(jnp.where(by_sub == lane, 1, 0), axis=0, keepdims=True)
    return [slot, first, last, present]


def kernel(
    dims,
    feat_ref, tiles_hbm, rows_s, cols_s, count_s, rows_v, cols_v, weight_ref, bias_ref, cot_ref, mask_ref,
    hidden_ref, gw_ref, gb_ref, gf_ref,
    tiles, tiles_t, source, prod, part, plane, grads, back, mate, stage, landed,
    table_v, table_s, wide, r0, h0, r1, q1, r2, q2, r3, q3, r4, full,
    tile_sem, table_sem,
    z_send, z_recv, c_send, c_recv, x_send, x_recv, g_send, g_recv, m_send, m_recv,
    a_send, a_recv, b_send, b_recv, d_send, d_recv, s_send, s_recv, e_send, e_recv,
):
    nz, n_col, slots, tb, width, group, scale = dims
    half = nz // 2
    piece = tb // PARTS
    row = lax.axis_index("row")
    col = lax.axis_index("col")
    z = row // 2
    core = row - 2 * z
    other = 1 - core
    far = nz // group
    z_up = lax.rem(z + 1, nz)
    z_down = lax.rem(z + nz - 1, nz)
    in_group = lax.rem(z, group)
    which_group = z // group

    def at_z(zz):
        return (2 * zz + core, col)

    mate_id = (2 * z + other, col)

    def peer(j):
        return lax.rem(col + j, n_col)

    def near_z(j):
        return which_group * group + lax.rem(in_group + j, group)

    def far_z(j):
        return lax.rem(which_group + j, far) * group + in_group

    load_tiles = pltpu.make_async_copy(tiles_hbm, tiles, tile_sem)
    load_tiles.start()

    barrier = pltpu.get_barrier_semaphore()

    def greet(who):
        pl.semaphore_signal(barrier, inc=1, device_id=who, device_id_type=MESH)

    greet(at_z(z_up))
    greet(at_z(z_down))
    greet(mate_id)

    @pl.loop(1, n_col)
    def _(j):
        greet((row, peer(j)))

    for j in range(1, group):
        greet(at_z(near_z(j)))
    for j in range(1, far):
        greet(at_z(far_z(j)))
    pl.semaphore_wait(barrier, 3 + (n_col - 1) + (group - 1) + (far - 1))

    def send(src, dst, send_sem, recv_sem, who):
        return pltpu.make_async_remote_copy(
            src_ref=src, dst_ref=dst, send_sem=send_sem, recv_sem=recv_sem, device_id=who, device_id_type=MESH
        )

    def rows_of(q):
        return pl.ds(q * piece, piece)

    def ring_copy(way, step, q):
        step_z = lax.rem(z + nz - step, nz) if way == 0 else lax.rem(z + step, nz)
        block = source.at[2 * step_z + core, rows_of(q)]
        who = at_z(z_up if way == 0 else z_down)
        return send(block, block, z_send.at[way, step, q], z_recv.at[way, step, q], who)

    def mate_copy(which, q):
        block = source.at[2 * which + core, rows_of(q)]
        return send(block, block, c_send.at[which, q], c_recv.at[which, q], mate_id)

    def takes(way, step, q, last):
        return step != last or (q < PARTS // 2) == (way == 0)

    source[row] = feat_ref[...]
    for q in range(PARTS):
        ring_copy(0, 0, q).start()
        ring_copy(1, 0, q).start()
    for q in range(PARTS):
        mate_copy(z, q).start()

    table_v[...] = jnp.zeros_like(table_v)
    table_v[0:1, 0:slots] = rows_v[...]
    table_v[1:2, 0:slots] = cols_v[...]
    live = lax.broadcasted_iota(jnp.int32, (1, tb), 1) < count_s[0, 0]
    row_key = jnp.where(live, table_v[0:1, :], tb)
    col_key = jnp.where(live, table_v[1:2, :], tb)
    lines = order_rows(row_key, tb) + order_rows(col_key, tb)
    for i, line in enumerate(lines):
        table_v[i : i + 1, :] = line
    save_table = pltpu.make_async_copy(table_v, table_s, table_sem)
    save_table.start()

    def ring_step(step, last):
        for q in range(PARTS):
            for way in (0, 1):
                if takes(way, last, q, 1):
                    ring_copy(way, step - 1, q).wait_recv()
                    came = lax.rem(z + nz - step, nz) if way == 0 else lax.rem(z + step, nz)
                    mate_copy(came, q).start()
                if last == 0:
                    ring_copy(way, step, q).start()

    @pl.loop(1, half - 1)
    def _(step):
        ring_step(step, 0)

    step = half - 1
    for q in range(PARTS):
        for way in (0, 1):
            ring_copy(way, step - 1, q).wait_recv()
            came = lax.rem(z + nz - step, nz) if way == 0 else lax.rem(z + step, nz)
            mate_copy(came, q).start()
            if takes(way, step, q, half - 1):
                ring_copy(way, step, q).start()

    load_tiles.wait()

    @pl.loop(0, slots)
    def _(s):
        tiles_t[s] = tiles[s].T

    save_table.wait()

    for q in range(PARTS):
        way = 0 if q < PARTS // 2 else 1
        ring_copy(way, half - 1, q).wait_recv()
        mate_copy(lax.rem(z + half, nz), q).start()

    @pl.loop(0, nz)
    def _(zz):
        for q in range(PARTS):
            block = source.at[2 * zz + other, rows_of(q)]
            send(block, block, c_send.at[zz, q], c_recv.at[zz, q], mate_id).wait_recv()

    def products(blocks, line, index_s, values):
        def one(k, total):
            slot = table_s[line, k]
            product = jnp.dot(blocks[slot], values[index_s[0, slot]], preferred_element_type=F32)
            total = jnp.where(table_s[line + 1, k] == 1, product, total + product)
            prod[k] = total
            return total

        lax.fori_loop(0, slots, one, jnp.zeros((tb, width), F32))

    def run_total(line, i):
        kept = table_s[line + 3, i] > 0
        return jnp.where(kept, prod[table_s[line + 2, i]], 0.0)

    products(tiles, 0, cols_s, source)

    def plane_copy(j):
        return send(part.at[peer(j)], plane.at[col], x_send.at[j], x_recv.at[j], (row, peer(j)))

    def plane_landed(j):
        back_col = lax.rem(col + n_col - j, n_col)
        return send(part.at[peer(j)], plane.at[back_col], x_send.at[j], x_recv.at[j], (row, peer(j)))

    @pl.loop(1, n_col)
    def _(j):
        part[peer(j)] = run_total(0, peer(j)).astype(BF16)
        plane_copy(j).start()

    def add_plane(j, total):
        plane_landed(j).wait_recv()
        return total + plane[lax.rem(col + n_col - j, n_col)].astype(F32)

    summed = lax.fori_loop(1, n_col, add_plane, run_total(0, col)).astype(BF16)

    pre_act = jnp.dot(summed, weight_ref[...], preferred_element_type=F32) + bias_ref[...]
    sigma = jax.nn.sigmoid(pre_act)
    hidden_ref[...] = (pre_act * sigma).astype(BF16)
    kept = jnp.broadcast_to(mask_ref[...].astype(F32), (tb, tb)).T
    kept = jnp.concatenate([kept] * (width // tb), axis=1)
    slope = sigma * (1.0 + pre_act * (1.0 - sigma))
    grad_pre = (cot_ref[...].astype(F32) * kept * slope).astype(BF16)
    grads[col] = lax.dot_general(
        grad_pre, weight_ref[...], (((1,), (1,)), ((), ())), preferred_element_type=F32
    ).astype(BF16)

    def grad_copy(j, source_col):
        block = grads.at[source_col]
        return send(block, block, g_send.at[j], g_recv.at[j], (row, peer(j)))

    @pl.loop(1, n_col)
    def _(j):
        grad_copy(j, col).start()

    wide[:, 0:width] = lax.dot_general(summed, grad_pre, (((0,), (0,)), ((), ())), preferred_element_type=F32)
    wide[:, width:] = lax.dot_general(
        grad_pre, jnp.ones((tb, tb), BF16), (((0,), (0,)), ((), ())), preferred_element_type=F32
    )
    share = width // 2
    slab = share // n_col
    split = send(wide.at[pl.ds(other * share, share)], r0, d_send.at[0], d_recv.at[0], mate_id)
    split.start()
    split.wait_recv()
    h0[...] = wide[pl.ds(pl.multiple_of(core * share, share), share), :] + r0[...]

    def slab_copy(j, source_col):
        rows = pl.ds(peer(j) * slab, slab)
        return send(h0.at[rows], r1.at[source_col], a_send.at[j], a_recv.at[j], (row, peer(j)))

    @pl.loop(1, n_col)
    def _(j):
        slab_copy(j, col).start()

    @pl.loop(1, n_col)
    def _(j):
        grad_copy(j, lax.rem(col + n_col - j, n_col)).wait_recv()

    def add_slab(j, total):
        back_col = lax.rem(col + n_col - j, n_col)
        slab_copy(j, back_col).wait_recv()
        return total + r1[back_col]

    own_slab = h0[pl.ds(pl.multiple_of(col * slab, slab), slab), :]
    q1[...] = lax.fori_loop(1, n_col, add_slab, own_slab)

    def near_copy(j, slot):
        return send(q1, r2.at[slot], b_send.at[j], b_recv.at[j], at_z(near_z(j)))

    def far_copy(j, slot):
        return send(q2, r3.at[slot], b_send.at[group + j], b_recv.at[group + j], at_z(far_z(j)))

    for j in range(1, group):
        near_copy(j, j).start()

    products(tiles_t, 4, rows_s, grads)

    def share_copy(zz, send_to_mate):
        src = back.at[2 * zz + (other if send_to_mate else core)]
        return send(src, mate.at[zz], m_send.at[zz], m_recv.at[zz], mate_id)

    def fill(zz):
        for which in (core, other):
            back[2 * zz + which] = run_total(4, 2 * zz + which).astype(BF16)
        share_copy(zz, True).start()

    fill(lax.rem(z + half, nz))

    @pl.loop(1, half)
    def _(step):
        fill(lax.rem(z + half - step, nz))
        fill(lax.rem(z + half + step, nz))

    fill(z)

    total = q1[...]
    for j in range(1, group):
        near_copy(j, j).wait_recv()
        total = total + r2[j]
    q2[...] = total
    for j in range(1, far):
        far_copy(j, j).start()

    def dest(way, step):
        return lax.rem(z + half - step, nz) if way == 0 else lax.rem(z + half + step, nz)

    def sum_copy(way, step, q):
        rows = rows_of(q)
        who = at_z(z_up if way == 0 else z_down)
        return send(
            stage.at[way, step, rows], landed.at[way, step, rows], s_send.at[way, step, q], s_recv.at[way, step, q], who
        )

    def mine(zz, q):
        rows = rows_of(q)
        return back[2 * zz + core, rows, :].astype(F32) + mate[zz, rows, :].astype(F32)

    def sum_step(way, step, q, has_more):
        rows = rows_of(q)
        total = mine(dest(way, step), q)
        if has_more:
            sum_copy(way, step - 1, q).wait_recv()
            total = total + landed[way, step - 1, rows, :].astype(F32)
        stage[way, step, rows, :] = total.astype(BF16)
        sum_copy(way, step, q).start()

    share_copy(dest(0, 0), False).wait_recv()
    for q in range(PARTS):
        sum_step(0 if q < PARTS // 2 else 1, 0, q, False)
    share_copy(dest(0, 1), False).wait_recv()
    share_copy(dest(1, 1), False).wait_recv()
    for q in range(PARTS):
        for way in (0, 1):
            sum_step(way, 1, q, (q < PARTS // 2) == (way == 0))

    def ring_sum(low, high):
        @pl.loop(low, high)
        def _(step):
            share_copy(dest(0, step), False).wait_recv()
            share_copy(dest(1, step), False).wait_recv()
            for q in range(PARTS):
                for way in (0, 1):
                    sum_step(way, step, q, True)

    middle = max(2, half // 2)
    late = max(middle, half - 1)
    ring_sum(2, middle)

    total = q2[...]
    for j in range(1, far):
        far_copy(j, j).wait_recv()
        total = total + r3[j]
    q3[...] = total * scale

    def done_copy(j, source_col):
        return send(q3, r4.at[pl.ds(source_col * slab, slab)], e_send.at[j], e_recv.at[j], (row, peer(j)))

    @pl.loop(1, n_col)
    def _(j):
        slab_copy(j, col).wait_send()
        done_copy(j, col).start()

    r4[pl.ds(pl.multiple_of(col * slab, slab), slab), :] = q3[...]
    ring_sum(middle, late)

    @pl.loop(1, n_col)
    def _(j):
        done_copy(j, lax.rem(col + n_col - j, n_col)).wait_recv()

    join = send(r4, full, d_send.at[1], d_recv.at[1], mate_id)
    join.start()
    ring_sum(late, half)

    share_copy(z, False).wait_recv()
    for q in range(PARTS):
        rows = rows_of(q)
        total = mine(z, q)
        for way in (0, 1):
            sum_copy(way, half - 1, q).wait_recv()
            total = total + landed[way, half - 1, rows, :].astype(F32)
        gf_ref[rows, :] = total.astype(BF16)

    join.wait_recv()
    split.wait_send()
    own_rows = pl.ds(pl.multiple_of(core * share, share), share)
    other_rows = pl.ds(pl.multiple_of(other * share, share), share)
    gw_ref[own_rows, :] = r4[:, 0:width]
    gw_ref[other_rows, :] = full[:, 0:width]
    wide[own_rows, 0:tb] = r4[:, width:]
    wide[other_rows, 0:tb] = full[:, width:]
    gb_ref[...] = wide[:, 0:tb].T[0:1, :]

    @pl.loop(0, half - 1)
    def _(step):
        for q in range(PARTS):
            for way in (0, 1):
                ring_copy(way, step, q).wait_send()

    for q in range(PARTS):
        ring_copy(0 if q < PARTS // 2 else 1, half - 1, q).wait_send()

    @pl.loop(0, nz)
    def _(zz):
        for q in range(PARTS):
            mate_copy(zz, q).wait_send()
        share_copy(zz, True).wait_send()

    @pl.loop(1, n_col)
    def _(j):
        plane_copy(j).wait_send()
        grad_copy(j, col).wait_send()
        done_copy(j, col).wait_send()

    join.wait_send()
    for j in range(1, group):
        near_copy(j, j).wait_send()
    for j in range(1, far):
        far_copy(j, j).wait_send()
    for q in range(PARTS):
        sum_copy(0 if q < PARTS // 2 else 1, 0, q).wait_send()

    @pl.loop(1, half)
    def _(step):
        for q in range(PARTS):
            for way in (0, 1):
                sum_copy(way, step, q).wait_send()


def on_device(
    features, tiles, tile_rows, tile_cols, tile_count, weight, bias, cotangent, label_mask
):
    n_row = lax.axis_size("row")
    n_col = lax.axis_size("col")
    nz = n_row // 2
    half = nz // 2
    group = 4 if nz >= 16 else 2
    far = nz // group
    tb = tiles.shape[-1]
    slots = tiles.shape[2]
    width = features.shape[2]
    share = width // 2
    slab = share // n_col
    lanes = width + tb
    scale = 1.0 / math.sqrt(n_row * n_col * tb)
    dims = (nz, n_col, slots, tb, width, group, scale)
    vmem = pl.BlockSpec(memory_space=pltpu.VMEM)
    smem = pl.BlockSpec(memory_space=pltpu.SMEM)
    dma = pltpu.SemaphoreType.DMA
    hidden, gw, gb, gf = pl.pallas_call(
        functools.partial(kernel, dims),
        out_shape=(
            jax.ShapeDtypeStruct((tb, width), BF16),
            jax.ShapeDtypeStruct((width, width), F32),
            jax.ShapeDtypeStruct((1, width), F32),
            jax.ShapeDtypeStruct((tb, width), BF16),
        ),
        in_specs=[vmem, pl.BlockSpec(memory_space=pl.ANY), smem, smem, smem] + [vmem] * 6,
        out_specs=(vmem,) * 4,
        scratch_shapes=[
            pltpu.VMEM((slots, tb, tb), BF16),
            pltpu.VMEM((slots, tb, tb), BF16),
            pltpu.VMEM((n_row, tb, width), BF16),
            pltpu.VMEM((slots, tb, width), F32),
            pltpu.VMEM((n_col, tb, width), BF16),
            pltpu.VMEM((n_col, tb, width), BF16),
            pltpu.VMEM((n_col, tb, width), BF16),
            pltpu.VMEM((n_row, tb, width), BF16),
            pltpu.VMEM((nz, tb, width), BF16),
            pltpu.VMEM((2, half, tb, width), BF16),
            pltpu.VMEM((2, half, tb, width), BF16),
            pltpu.VMEM((8, tb), jnp.int32),
            pltpu.SMEM((8, tb), jnp.int32),
            pltpu.VMEM((width, lanes), F32),
            pltpu.VMEM((share, lanes), F32),
            pltpu.VMEM((share, lanes), F32),
            pltpu.VMEM((n_col, slab, lanes), F32),
            pltpu.VMEM((slab, lanes), F32),
            pltpu.VMEM((group, slab, lanes), F32),
            pltpu.VMEM((slab, lanes), F32),
            pltpu.VMEM((far, slab, lanes), F32),
            pltpu.VMEM((slab, lanes), F32),
            pltpu.VMEM((share, lanes), F32),
            pltpu.VMEM((share, lanes), F32),
            dma, dma,
            dma((2, half, PARTS)), dma((2, half, PARTS)),
            dma((nz, PARTS)), dma((nz, PARTS)),
            dma((n_col,)), dma((n_col,)),
            dma((n_col,)), dma((n_col,)),
            dma((nz,)), dma((nz,)),
            dma((n_col,)), dma((n_col,)),
            dma((group + far,)), dma((group + far,)),
            dma((2,)), dma((2,)),
            dma((2, half, PARTS)), dma((2, half, PARTS)),
            dma((n_col,)), dma((n_col,)),
        ],
        compiler_params=pltpu.CompilerParams(
            collective_id=0, has_side_effects=True, vmem_limit_bytes=56 << 20
        ),
        name="graph_layer",
    )(
        features[0], tiles[0, 0], tile_rows[0], tile_cols[0], tile_count,
        tile_rows[0], tile_cols[0], weight, bias[None], cotangent[0], label_mask,
    )
    return hidden[None], gw, gb[0], gf[None]


def solution(mesh):
    return jax.shard_map(
        on_device,
        mesh=mesh,
        in_specs=(
            P("col", "row", None),
            P("row", "col", None, None, None),
            P("row", "col", None),
            P("row", "col", None),
            P("row", "col"),
            P(),
            P(),
            P("row", "col", None),
            P("row", "col"),
        ),
        out_specs=(P("row", "col", None), P(), P(), P("col", "row", None)),
        check_vma=False,
    )
```

```python
import functools
import math

import jax
import jax.numpy as jnp
from jax import lax
from jax.experimental import pallas as pl
from jax.experimental.pallas import tpu as pltpu
from jax.sharding import PartitionSpec as P

MESH = pl.DeviceIdType.MESH
PARTS = 4
UNROLL = 8
F32 = jnp.float32
BF16 = jnp.bfloat16


def order_rows(key, limit):
    size = key.shape[1]
    by_lane = jnp.broadcast_to(key, (size, size))
    by_sub = by_lane.T
    lane = lax.broadcasted_iota(jnp.int32, (size, size), 1)
    sub = lax.broadcasted_iota(jnp.int32, (size, size), 0)
    same_before = jnp.where(by_sub == by_lane, jnp.where(sub < lane, 1, 0), 0)
    before = jnp.where(by_sub < by_lane, 1, same_before)
    rank = jnp.sum(before, axis=0, keepdims=True)
    repeats = jnp.sum(same_before, axis=0, keepdims=True)
    rank_sub = jnp.broadcast_to(rank, (size, size)).T
    repeats_sub = jnp.broadcast_to(repeats, (size, size)).T
    here = rank_sub == lane
    slot = jnp.sum(jnp.where(here, sub, 0), axis=0, keepdims=True)
    first = jnp.sum(jnp.where(here, jnp.where(repeats_sub == 0, 1, 0), 0), axis=0, keepdims=True)
    last = jnp.sum(jnp.where(by_sub <= lane, 1, 0), axis=0, keepdims=True) - 1
    last = jnp.maximum(last, 0)
    present = jnp.sum(jnp.where(by_sub == lane, 1, 0), axis=0, keepdims=True)
    return [slot, first, last, present]


def kernel(
    dims,
    feat_ref, tiles_hbm, rows_s, cols_s, count_s, rows_v, cols_v, weight_ref, bias_ref, cot_ref, mask_ref,
    hidden_ref, gw_ref, gb_ref, gf_ref,
    tiles, tiles_t, source, prod, part, plane, grads, back, mate, stage, landed,
    table_v, table_s, wide, r0, h0, r1, q1, r2, q2, r3, q3, r4, full,
    tile_sem, table_sem,
    z_send, z_recv, c_send, c_recv, x_send, x_recv, g_send, g_recv, m_send, m_recv,
    a_send, a_recv, b_send, b_recv, d_send, d_recv, s_send, s_recv, e_send, e_recv,
):
    nz, n_col, slots, tb, width, group, scale = dims
    half = nz // 2
    piece = tb // PARTS
    row = lax.axis_index("row")
    col = lax.axis_index("col")
    z = row // 2
    core = row - 2 * z
    other = 1 - core
    far = nz // group
    z_up = lax.rem(z + 1, nz)
    z_down = lax.rem(z + nz - 1, nz)
    in_group = lax.rem(z, group)
    which_group = z // group

    def at_z(zz):
        return (2 * zz + core, col)

    mate_id = (2 * z + other, col)

    def peer(j):
        return lax.rem(col + j, n_col)

    def near_z(j):
        return which_group * group + lax.rem(in_group + j, group)

    def far_z(j):
        return lax.rem(which_group + j, far) * group + in_group

    load_tiles = pltpu.make_async_copy(tiles_hbm, tiles, tile_sem)
    load_tiles.start()

    barrier = pltpu.get_barrier_semaphore()

    def greet(who):
        pl.semaphore_signal(barrier, inc=1, device_id=who, device_id_type=MESH)

    greet(at_z(z_up))
    greet(at_z(z_down))
    greet(mate_id)

    @pl.loop(1, n_col)
    def _(j):
        greet((row, peer(j)))

    pl.semaphore_wait(barrier, 3 + (n_col - 1))

    def send(src, dst, send_sem, recv_sem, who):
        return pltpu.make_async_remote_copy(
            src_ref=src, dst_ref=dst, send_sem=send_sem, recv_sem=recv_sem, device_id=who, device_id_type=MESH
        )

    def rows_of(q):
        return pl.ds(q * piece, piece)

    def ring_copy(way, step, q):
        step_z = lax.rem(z + nz - step, nz) if way == 0 else lax.rem(z + step, nz)
        block = source.at[2 * step_z + core, rows_of(q)]
        who = at_z(z_up if way == 0 else z_down)
        return send(block, block, z_send.at[way, step, q], z_recv.at[way, step, q], who)

    def mate_copy(which, q):
        block = source.at[2 * which + core, rows_of(q)]
        return send(block, block, c_send.at[which, q], c_recv.at[which, q], mate_id)

    def takes(way, step, q, last):
        return step != last or (q < PARTS // 2) == (way == 0)

    source[row] = feat_ref[...]
    for q in range(PARTS):
        ring_copy(0, 0, q).start()
        ring_copy(1, 0, q).start()
    for q in range(PARTS):
        mate_copy(z, q).start()

    table_v[...] = jnp.zeros_like(table_v)
    table_v[0:1, 0:slots] = rows_v[...]
    table_v[1:2, 0:slots] = cols_v[...]
    live = lax.broadcasted_iota(jnp.int32, (1, tb), 1) < count_s[0, 0]
    row_key = jnp.where(live, table_v[0:1, :], tb)
    col_key = jnp.where(live, table_v[1:2, :], tb)
    lines = order_rows(row_key, tb) + order_rows(col_key, tb)
    for i, line in enumerate(lines):
        table_v[i : i + 1, :] = line
    save_table = pltpu.make_async_copy(table_v, table_s, table_sem)
    save_table.start()

    def ring_step(step, last):
        for q in range(PARTS):
            for way in (0, 1):
                if takes(way, last, q, 1):
                    ring_copy(way, step - 1, q).wait_recv()
                    came = lax.rem(z + nz - step, nz) if way == 0 else lax.rem(z + step, nz)
                    mate_copy(came, q).start()
                if last == 0:
                    ring_copy(way, step, q).start()

    @pl.loop(1, half - 1)
    def _(step):
        ring_step(step, 0)

    step = half - 1
    for q in range(PARTS):
        for way in (0, 1):
            ring_copy(way, step - 1, q).wait_recv()
            came = lax.rem(z + nz - step, nz) if way == 0 else lax.rem(z + step, nz)
            mate_copy(came, q).start()
            if takes(way, step, q, half - 1):
                ring_copy(way, step, q).start()

    load_tiles.wait()

    @pl.loop(0, slots)
    def _(s):
        tiles_t[s] = tiles[s].T

    save_table.wait()

    for q in range(PARTS):
        way = 0 if q < PARTS // 2 else 1
        ring_copy(way, half - 1, q).wait_recv()
        mate_copy(lax.rem(z + half, nz), q).start()

    @pl.loop(0, nz)
    def _(zz):
        for q in range(PARTS):
            block = source.at[2 * zz + other, rows_of(q)]
            send(block, block, c_send.at[zz, q], c_recv.at[zz, q], mate_id).wait_recv()

    def products(blocks, line, index_s, values):
        def some(turn, total):
            for i in range(UNROLL):
                k = turn * UNROLL + i
                slot = table_s[line, k]
                product = jnp.dot(blocks[slot], values[index_s[0, slot]], preferred_element_type=F32)
                total = jnp.where(table_s[line + 1, k] == 1, product, total + product)
                prod[k] = total
            return total

        lax.fori_loop(0, slots // UNROLL, some, jnp.zeros((tb, width), F32))

    def run_total(line, i):
        kept = table_s[line + 3, i] > 0
        return jnp.where(kept, prod[table_s[line + 2, i]], 0.0)

    products(tiles, 0, cols_s, source)

    def plane_copy(j):
        return send(part.at[peer(j)], plane.at[col], x_send.at[j], x_recv.at[j], (row, peer(j)))

    def plane_landed(j):
        back_col = lax.rem(col + n_col - j, n_col)
        return send(part.at[peer(j)], plane.at[back_col], x_send.at[j], x_recv.at[j], (row, peer(j)))

    @pl.loop(1, n_col)
    def _(j):
        part[peer(j)] = run_total(0, peer(j)).astype(BF16)
        plane_copy(j).start()

    def add_plane(j, total):
        plane_landed(j).wait_recv()
        return total + plane[lax.rem(col + n_col - j, n_col)].astype(F32)

    summed = lax.fori_loop(1, n_col, add_plane, run_total(0, col)).astype(BF16)

    pre_act = jnp.dot(summed, weight_ref[...], preferred_element_type=F32) + bias_ref[...]
    sigma = jax.nn.sigmoid(pre_act)
    hidden_ref[...] = (pre_act * sigma).astype(BF16)
    kept = jnp.broadcast_to(mask_ref[...].astype(F32), (tb, tb)).T
    kept = jnp.concatenate([kept] * (width // tb), axis=1)
    slope = sigma * (1.0 + pre_act * (1.0 - sigma))
    grad_pre = (cot_ref[...].astype(F32) * kept * slope).astype(BF16)
    grads[col] = lax.dot_general(
        grad_pre, weight_ref[...], (((1,), (1,)), ((), ())), preferred_element_type=F32
    ).astype(BF16)

    def grad_copy(j, source_col):
        block = grads.at[source_col]
        return send(block, block, g_send.at[j], g_recv.at[j], (row, peer(j)))

    @pl.loop(1, n_col)
    def _(j):
        grad_copy(j, col).start()

    wide[:, 0:width] = lax.dot_general(summed, grad_pre, (((0,), (0,)), ((), ())), preferred_element_type=F32)
    wide[:, width:] = lax.dot_general(
        grad_pre, jnp.ones((tb, tb), BF16), (((0,), (0,)), ((), ())), preferred_element_type=F32
    )
    share = width // 2
    slab = share // n_col
    split = send(wide.at[pl.ds(other * share, share)], r0, d_send.at[0], d_recv.at[0], mate_id)
    split.start()
    split.wait_recv()
    h0[...] = wide[pl.ds(pl.multiple_of(core * share, share), share), :] + r0[...]

    def slab_copy(j, source_col):
        rows = pl.ds(peer(j) * slab, slab)
        return send(h0.at[rows], r1.at[source_col], a_send.at[j], a_recv.at[j], (row, peer(j)))

    @pl.loop(1, n_col)
    def _(j):
        slab_copy(j, col).start()

    @pl.loop(1, n_col)
    def _(j):
        grad_copy(j, lax.rem(col + n_col - j, n_col)).wait_recv()

    products(tiles_t, 4, rows_s, grads)

    def share_copy(zz, send_to_mate):
        src = back.at[2 * zz + (other if send_to_mate else core)]
        return send(src, mate.at[zz], m_send.at[zz], m_recv.at[zz], mate_id)

    def fill(zz):
        for which in (core, other):
            back[2 * zz + which] = run_total(4, 2 * zz + which).astype(BF16)
        share_copy(zz, True).start()

    def add_slab(j, total):
        back_col = lax.rem(col + n_col - j, n_col)
        slab_copy(j, back_col).wait_recv()
        return total + r1[back_col]

    own_slab = h0[pl.ds(pl.multiple_of(col * slab, slab), slab), :]
    q1[...] = lax.fori_loop(1, n_col, add_slab, own_slab)

    def near_copy(j, slot):
        return send(q1, r2.at[slot], b_send.at[j], b_recv.at[j], at_z(near_z(j)))

    def far_copy(j, slot):
        return send(q2, r3.at[slot], b_send.at[group + j], b_recv.at[group + j], at_z(far_z(j)))

    for j in range(1, group):
        near_copy(j, j).start()

    def dest(way, step):
        return lax.rem(z + half - step, nz) if way == 0 else lax.rem(z + half + step, nz)

    def sum_copy(way, step, q):
        rows = rows_of(q)
        who = at_z(z_up if way == 0 else z_down)
        return send(
            stage.at[way, step, rows], landed.at[way, step, rows], s_send.at[way, step, q], s_recv.at[way, step, q], who
        )

    def mine(zz, q):
        rows = rows_of(q)
        return back[2 * zz + core, rows, :].astype(F32) + mate[zz, rows, :].astype(F32)

    def sum_step(way, step, q, has_more):
        rows = rows_of(q)
        total = mine(dest(way, step), q)
        if has_more:
            sum_copy(way, step - 1, q).wait_recv()
            total = total + landed[way, step - 1, rows, :].astype(F32)
        stage[way, step, rows, :] = total.astype(BF16)
        sum_copy(way, step, q).start()

    def ring_sum(low, high):
        @pl.loop(low, high)
        def _(step):
            fill(dest(0, step + 2))
            fill(dest(1, step + 2))
            share_copy(dest(0, step), False).wait_recv()
            share_copy(dest(1, step), False).wait_recv()
            for q in range(PARTS):
                for way in (0, 1):
                    sum_step(way, step, q, True)

    def ring_tail(step):
        if step == half - 2:
            fill(z)
        share_copy(dest(0, step), False).wait_recv()
        share_copy(dest(1, step), False).wait_recv()
        for q in range(PARTS):
            for way in (0, 1):
                sum_step(way, step, q, True)

    fill(dest(0, 0))
    fill(dest(0, 1))
    fill(dest(1, 1))
    share_copy(dest(0, 0), False).wait_recv()
    for q in range(PARTS):
        sum_step(0 if q < PARTS // 2 else 1, 0, q, False)
    fill(dest(0, 2))
    fill(dest(1, 2))
    fill(dest(0, 3))
    fill(dest(1, 3))
    share_copy(dest(0, 1), False).wait_recv()
    share_copy(dest(1, 1), False).wait_recv()
    for q in range(PARTS):
        for way in (0, 1):
            sum_step(way, 1, q, (q < PARTS // 2) == (way == 0))

    total = q1[...]
    for j in range(1, group):
        near_copy(j, j).wait_recv()
        total = total + r2[j]
    q2[...] = total
    for j in range(1, far):
        far_copy(j, j).start()

    middle = max(2, half // 2 + 1)
    ring_sum(2, middle)

    total = q2[...]
    for j in range(1, far):
        far_copy(j, j).wait_recv()
        total = total + r3[j]
    q3[...] = total * scale

    def done_copy(j, source_col):
        return send(q3, r4.at[pl.ds(source_col * slab, slab)], e_send.at[j], e_recv.at[j], (row, peer(j)))

    @pl.loop(1, n_col)
    def _(j):
        slab_copy(j, col).wait_send()
        done_copy(j, col).start()

    r4[pl.ds(pl.multiple_of(col * slab, slab), slab), :] = q3[...]
    ring_sum(middle, half - 2)
    ring_tail(half - 2)
    ring_tail(half - 1)

    @pl.loop(1, n_col)
    def _(j):
        done_copy(j, lax.rem(col + n_col - j, n_col)).wait_recv()

    join = send(r4, full, d_send.at[1], d_recv.at[1], mate_id)
    join.start()

    share_copy(z, False).wait_recv()
    for q in range(PARTS):
        rows = rows_of(q)
        total = mine(z, q)
        for way in (0, 1):
            sum_copy(way, half - 1, q).wait_recv()
            total = total + landed[way, half - 1, rows, :].astype(F32)
        gf_ref[rows, :] = total.astype(BF16)

    join.wait_recv()
    split.wait_send()
    own_rows = pl.ds(pl.multiple_of(core * share, share), share)
    other_rows = pl.ds(pl.multiple_of(other * share, share), share)
    gw_ref[own_rows, :] = r4[:, 0:width]
    gw_ref[other_rows, :] = full[:, 0:width]
    wide[own_rows, 0:tb] = r4[:, width:]
    wide[other_rows, 0:tb] = full[:, width:]
    gb_ref[...] = wide[:, 0:tb].T[0:1, :]

    @pl.loop(0, half - 1)
    def _(step):
        for q in range(PARTS):
            for way in (0, 1):
                ring_copy(way, step, q).wait_send()

    for q in range(PARTS):
        ring_copy(0 if q < PARTS // 2 else 1, half - 1, q).wait_send()

    @pl.loop(0, nz)
    def _(zz):
        for q in range(PARTS):
            mate_copy(zz, q).wait_send()
        share_copy(zz, True).wait_send()

    @pl.loop(1, n_col)
    def _(j):
        plane_copy(j).wait_send()
        grad_copy(j, col).wait_send()
        done_copy(j, col).wait_send()

    join.wait_send()
    for j in range(1, group):
        near_copy(j, j).wait_send()
    for j in range(1, far):
        far_copy(j, j).wait_send()
    for q in range(PARTS):
        sum_copy(0 if q < PARTS // 2 else 1, 0, q).wait_send()

    @pl.loop(1, half)
    def _(step):
        for q in range(PARTS):
            for way in (0, 1):
                sum_copy(way, step, q).wait_send()


def hand_over(hidden_in, gw_in, gb_in, gf_in, hidden_ref, gw_ref, gb_ref, gf_ref):
    hidden_ref[...] = hidden_in[...]
    gw_ref[...] = gw_in[...]
    gb_ref[...] = gb_in[...]
    gf_ref[...] = gf_in[...]


def on_device(
    features, tiles, tile_rows, tile_cols, tile_count, weight, bias, cotangent, label_mask
):
    n_row = lax.axis_size("row")
    n_col = lax.axis_size("col")
    nz = n_row // 2
    half = nz // 2
    group = 4 if nz >= 16 else 2
    far = nz // group
    tb = tiles.shape[-1]
    slots = tiles.shape[2]
    width = features.shape[2]
    share = width // 2
    slab = share // n_col
    lanes = width + tb
    scale = 1.0 / math.sqrt(n_row * n_col * tb)
    dims = (nz, n_col, slots, tb, width, group, scale)
    vmem = pl.BlockSpec(memory_space=pltpu.VMEM)
    smem = pl.BlockSpec(memory_space=pltpu.SMEM)
    dma = pltpu.SemaphoreType.DMA
    hidden, gw, gb, gf = pl.pallas_call(
        functools.partial(kernel, dims),
        out_shape=(
            jax.ShapeDtypeStruct((tb, width), BF16),
            jax.ShapeDtypeStruct((width, width), F32),
            jax.ShapeDtypeStruct((1, width), F32),
            jax.ShapeDtypeStruct((tb, width), BF16),
        ),
        in_specs=[vmem, pl.BlockSpec(memory_space=pl.ANY), smem, smem, smem] + [vmem] * 6,
        out_specs=(vmem,) * 4,
        scratch_shapes=[
            pltpu.VMEM((slots, tb, tb), BF16),
            pltpu.VMEM((slots, tb, tb), BF16),
            pltpu.VMEM((n_row, tb, width), BF16),
            pltpu.VMEM((slots, tb, width), F32),
            pltpu.VMEM((n_col, tb, width), BF16),
            pltpu.VMEM((n_col, tb, width), BF16),
            pltpu.VMEM((n_col, tb, width), BF16),
            pltpu.VMEM((n_row, tb, width), BF16),
            pltpu.VMEM((nz, tb, width), BF16),
            pltpu.VMEM((2, half, tb, width), BF16),
            pltpu.VMEM((2, half, tb, width), BF16),
            pltpu.VMEM((8, tb), jnp.int32),
            pltpu.SMEM((8, tb), jnp.int32),
            pltpu.VMEM((width, lanes), F32),
            pltpu.VMEM((share, lanes), F32),
            pltpu.VMEM((share, lanes), F32),
            pltpu.VMEM((n_col, slab, lanes), F32),
            pltpu.VMEM((slab, lanes), F32),
            pltpu.VMEM((group, slab, lanes), F32),
            pltpu.VMEM((slab, lanes), F32),
            pltpu.VMEM((far, slab, lanes), F32),
            pltpu.VMEM((slab, lanes), F32),
            pltpu.VMEM((share, lanes), F32),
            pltpu.VMEM((share, lanes), F32),
            dma, dma,
            dma((2, half, PARTS)), dma((2, half, PARTS)),
            dma((nz, PARTS)), dma((nz, PARTS)),
            dma((n_col,)), dma((n_col,)),
            dma((n_col,)), dma((n_col,)),
            dma((nz,)), dma((nz,)),
            dma((n_col,)), dma((n_col,)),
            dma((group + far,)), dma((group + far,)),
            dma((2,)), dma((2,)),
            dma((2, half, PARTS)), dma((2, half, PARTS)),
            dma((n_col,)), dma((n_col,)),
        ],
        compiler_params=pltpu.CompilerParams(
            collective_id=0, has_side_effects=True, vmem_limit_bytes=63 << 20
        ),
        name="graph_layer",
    )(
        features[0], tiles[0, 0], tile_rows[0], tile_cols[0], tile_count,
        tile_rows[0], tile_cols[0], weight, bias[None], cotangent[0], label_mask,
    )
    hidden, gw, gb, gf = pl.pallas_call(
        hand_over,
        out_shape=tuple(jax.ShapeDtypeStruct(x.shape, x.dtype) for x in (hidden, gw, gb, gf)),
        in_specs=[vmem] * 4,
        out_specs=(vmem,) * 4,
        compiler_params=pltpu.CompilerParams(vmem_limit_bytes=63 << 20),
        name="hand_over",
    )(hidden, gw, gb, gf)
    return hidden[None], gw, gb[0], gf[None]


def solution(mesh):
    return jax.shard_map(
        on_device,
        mesh=mesh,
        in_specs=(
            P("col", "row", None),
            P("row", "col", None, None, None),
            P("row", "col", None),
            P("row", "col", None),
            P("row", "col"),
            P(),
            P(),
            P("row", "col", None),
            P("row", "col"),
        ),
        out_specs=(P("row", "col", None), P(), P(), P("col", "row", None)),
        check_vma=False,
    )
```
